32 devices in a mesh: row: 8 (over y, x, core), col: 4 (over z).
Axes of the slice: x: 2, y: 2, z: 4, core: 2. Of those that a mesh axis runs over, the one named last changes fastest.
Arguments:
- trailing: float32 [4096, 8192], P('row', 'col'), may hold values from -6 to 6
- leaf_v: float32 [4096, 256], P(('row', 'col')), may hold values from -0.25 to 0.25
- leaf_t: float32 [2048, 256], P(('row', 'col')), may hold values from -0.375 to 0.375
- tree_y: float32 [2048, 256], P(('row', 'col')), may hold values from -0.375 to 0.375
- tree_t: float32 [2048, 256], P(('row', 'col')), may hold values from -0.1875 to 0.1875
Outputs:
- updated: float32 [4096, 8192], P('row', 'col')
The draws below stay inside these ranges and needn't reach their ends.
All inputs are finite; a program needn't handle non-finite values.
Results may differ from the reference program's by a relative error of at most 0.00016.
Values sent between devices are 32-bit elements; how exact they have to be, the bound alone decides.
No kernel may reach another device: no remote copies, remote signals or barrier semaphores. Data moves between devices by JAX's collectives and lax.ppermute only.
A program may use at most 64 MiB of HBM per device.

```python
import jax
import jax.numpy as jnp
from jax import lax

B = 256
RD = 512
M = 4096
N = 8192
LEVELS = 3
N_ROW = 8


def block_levels(key, shape, pieces, smallest, top_value):
    def one(axis_at, parts):
        steps = jax.random.uniform(jax.random.fold_in(jax.random.fold_in(key, 6), axis_at), (parts,), jnp.float32, smallest / len(pieces), top_value / len(pieces))
        return jnp.repeat(jnp.exp(steps), shape[axis_at] // parts).reshape((-1,) + (1,) * (len(shape) - axis_at - 1))

    factor_of = one(*pieces[0])
    for cut in pieces[1:]:
        factor_of = factor_of * one(*cut)
    return factor_of


def noise(rng, shape, scale, bound, shards=(), held_as=jnp.bfloat16):
    gain = block_levels(rng, shape, shards, -0.22, 0.18) if shards else 1.0
    array = jax.random.normal(rng, shape, jnp.float32) * scale * gain
    return jnp.minimum(jnp.maximum(array, -bound), bound).astype(held_as)


def setup_inputs(seed: int = 0) -> dict:
    arg_keys = jax.random.split(jax.random.key(seed), 6)
    return {
        "trailing": noise(arg_keys[0], (M, N), 1.0, 6.0, ((0, 8), (1, 4)), jnp.float32),
        "leaf_v": noise(arg_keys[1], (M, B), RD ** -0.5, 0.25, ((0, 32),), jnp.float32),
        "leaf_t": noise(arg_keys[2], (N_ROW * B, B), B ** -0.5, 0.375, ((0, 32),), jnp.float32),
        "tree_y": noise(arg_keys[3], (N_ROW * B, B), B ** -0.5, 0.375, ((0, 32),), jnp.float32),
        "tree_t": noise(arg_keys[4], (N_ROW * B, B), (4 * B) ** -0.5, 0.1875, ((0, 32),), jnp.float32),
    }


def product(left, right):
    return jnp.dot(left, right, precision=lax.Precision.HIGHEST, preferred_element_type=jnp.float32)


def reference(trailing, leaf_v, leaf_t, tree_y, tree_t):
    height = trailing.shape[0] // N_ROW
    blocks = []
    for index in range(N_ROW):
        block = trailing[index * height:(index + 1) * height]
        vectors = leaf_v[index * height:(index + 1) * height]
        coeffs = leaf_t[index * B:(index + 1) * B]
        inner = product(vectors.T, block)
        blocks.append(block - product(vectors, product(coeffs.T, inner)))
    tops = [block[:B] for block in blocks]
    for level in range(LEVELS):
        stride = 1 << level
        fresh = list(tops)
        for upper in range(N_ROW):
            if (upper // stride) % 2 == 0:
                lower = upper + stride
                lower_y = tree_y[lower * B:(lower + 1) * B]
                upper_t = tree_t[upper * B:(upper + 1) * B]
                coeff_rows = product(upper_t.T, tops[upper] + product(lower_y.T, tops[lower]))
                fresh[upper] = tops[upper] - coeff_rows
                fresh[lower] = tops[lower] - product(lower_y, coeff_rows)
        tops = fresh
    return jnp.concatenate([jnp.concatenate([tops[index], blocks[index][B:]], axis=0) for index in range(N_ROW)], axis=0)
```

```python
import functools

import jax
import jax.numpy as jnp
from jax import lax
from jax.experimental import pallas as pl
from jax.experimental.pallas import tpu as pltpu
from jax.sharding import PartitionSpec as P

CHUNKS = 4
F32, BF16 = jnp.float32, jnp.bfloat16
VMEM = pl.BlockSpec(memory_space=pltpu.VMEM)
SMEM = pl.BlockSpec(memory_space=pltpu.SMEM)


def swap(value, axis, mask):
    return lax.ppermute(value, axis, [(i, i ^ mask) for i in range(lax.axis_size(axis))])


def spread(piece, axis):
    return [piece] + [swap(piece, axis, k) for k in range(1, lax.axis_size(axis))]


def split(x):
    high = x.astype(BF16)
    return high, (x - high.astype(F32)).astype(BF16)


def dot3(ah, al, bh, bl, dims=((1,), (0,))):
    d = functools.partial(lax.dot_general, dimension_numbers=(dims, ((), ())), preferred_element_type=F32)
    return d(ah, bh) + (d(ah, bl) + d(al, bh))


def dotf(a, b, dims=((1,), (0,))):
    return dot3(*split(a), *split(b), dims)


def place(index_ref, pieces, offset, rows, out):
    own = index_ref[1]
    for k, piece in enumerate(pieces):
        out[pl.ds(pl.multiple_of((own ^ k) * rows, rows), rows), :] = piece[offset:offset + rows, :]


def leaf_factors(n, vr, tr, index_ref, *refs):
    pieces, (vth, vtl, ph, plo, block), (v, t) = refs[:n], refs[n:n + 5], refs[n + 5:]
    place(index_ref, pieces, 0, vr, v)
    place(index_ref, pieces, vr, tr, t)
    place(index_ref, pieces, vr + tr, tr, block)
    full = v[...]
    vth[...], vtl[...] = split(full.T)
    ph[...], plo[...] = split(dotf(full, t[...], ((1,), (1,))))


def level_factors(level, n, tr, offset, index_ref, *refs):
    width = refs[-1].shape[0]
    own, far = refs[-2:]
    fh, fl = refs[-4:-2]
    first, second, pieces = refs[0], refs[1], refs[2:2 + n]
    place(index_ref, pieces, offset, tr, far)
    row = index_ref[0]
    bit = (row >> level) & 1

    @pl.when(bit == (row & 1))
    def _():
        own[...] = first[...]

    @pl.when(bit != (row & 1))
    def _():
        own[...] = second[...]

    form_factors(width, bit, own, far, fh, fl)


def form_factors(width, bit, own, far, fh, fl):
    @pl.when(bit == 0)
    def _():
        s, y = own[...], far[...]
        fh[:, :width], fl[:, :width] = split(s.T)
        fh[:, width:], fl[:, width:] = split(dotf(y, s).T)

    @pl.when(bit == 1)
    def _():
        y, s = own[...], far[...]
        ys = dotf(y, s, ((1,), (1,)))
        fh[:, width:], fl[:, width:] = split(ys)
        fh[:, :width], fl[:, :width] = split(dotf(ys, y, ((1,), (1,))))


def first_factors(index_ref, own, far, fh, fl):
    form_factors(own.shape[0], index_ref[0] & 1, own, far, fh, fl)


def second_block(n, tr, index_ref, *refs):
    place(index_ref, refs[:n], 0, tr, refs[n])


def leaf_apply(width, c, vth, vtl, ph, plo, _, top, rest):
    block = c[...]
    ih, il = split(dot3(vth[...], vtl[...], *split(block)))
    change = dot3(ph[...], plo[...], ih, il)
    top[...] = block[:width] - change[:width]
    rest[...] = block[width:] - change[width:]


def level_apply(width, own, far, fh, fl, *refs):
    out = refs[-1]
    mine = own[...]
    oh, ol = split(mine)
    xh, xl = split(far[...])
    change = dot3(fh[:, :width], fl[:, :width], oh, ol) + dot3(fh[:, width:], fl[:, width:], xh, xl)
    out[...] = mine - change


def cost(flops, size):
    return pl.CostEstimate(flops=flops, bytes_accessed=size, transcendentals=0)


def per_device(trailing, leaf_v, leaf_t, tree_y, tree_t):
    height, columns = trailing.shape
    width = leaf_v.shape[1]
    vr, tr = leaf_v.shape[0], leaf_t.shape[0]
    n = lax.axis_size("col")
    depth = lax.axis_size("row").bit_length() - 1
    row = lax.axis_index("row")
    index = jnp.stack([row, lax.axis_index("col")]).astype(jnp.int32)
    small = jax.ShapeDtypeStruct((width, width), F32)
    pair = [jax.ShapeDtypeStruct((width, 2 * width), BF16)] * 2
    scratch = pltpu.VMEM((width, width), F32)

    def role(level, flip=False):
        return jnp.where((row >> level & 1 == 1) != flip, tree_y, tree_t)

    group0 = jnp.concatenate([leaf_v, leaf_t, role(0)], axis=0)
    far_shards = [swap(role(level), "row", 1 << level) for level in range(1, depth)]
    pieces0 = spread(group0, "col")
    vth, vtl, ph, plo, block0 = pl.pallas_call(
        functools.partial(leaf_factors, n, vr, tr),
        out_shape=[jax.ShapeDtypeStruct((width, height), BF16)] * 2 + [jax.ShapeDtypeStruct((height, width), BF16)] * 2 + [small],
        in_specs=[SMEM] + [VMEM] * n,
        out_specs=[VMEM] * 5,
        scratch_shapes=[pltpu.VMEM((height, width), F32), scratch],
        name="leaf_factors",
    )(index, *pieces0)
    far0 = swap(block0, "row", 1)
    factors = [
        pl.pallas_call(first_factors, out_shape=pair, in_specs=[SMEM] + [VMEM] * 2, out_specs=[VMEM] * 2, name="factors0")(
            index, block0, far0
        )
    ]
    group1 = jnp.concatenate([role(0, True), far_shards[0]], axis=0)
    group2 = jnp.concatenate(far_shards[1:], axis=0)
    group1, pieces0[1:] = lax.optimization_barrier((group1, pieces0[1:]))
    pieces1 = spread(group1, "col")
    group2, pieces1[1:] = lax.optimization_barrier((group2, pieces1[1:]))
    pieces2 = spread(group2, "col")
    block1 = pl.pallas_call(
        functools.partial(second_block, n, tr), out_shape=small, in_specs=[SMEM] + [VMEM] * n, out_specs=VMEM, name="block1"
    )(index, *pieces1)
    for level in range(1, depth):
        pieces, offset = (pieces1, tr) if level == 1 else (pieces2, (level - 2) * tr)
        factors.append(
            pl.pallas_call(
                functools.partial(level_factors, level, n, tr, offset),
                out_shape=pair,
                in_specs=[SMEM] + [VMEM] * (2 + n),
                out_specs=[VMEM] * 2,
                scratch_shapes=[scratch, scratch],
                name=f"factors{level}",
            )(index, block0, block1, *pieces)
        )

    part = columns // CHUNKS
    chunk = jax.ShapeDtypeStruct((width, part), F32)
    whole = jax.ShapeDtypeStruct((height, columns), F32)
    out = None
    tops = []
    for i in range(CHUNKS):
        at = functools.partial(lambda i, *_: (0, i), i)
        below = functools.partial(lambda i, *_: (1, i), i)
        held = [pl.BlockSpec(a.shape, lambda *_: (0, 0)) for a in (vth, vtl, ph, plo)]
        extra = trailing if out is None else out
        top, out = pl.pallas_call(
            functools.partial(leaf_apply, width),
            grid=(1,),
            out_shape=[chunk, whole],
            in_specs=[pl.BlockSpec((height, part), at)] + held + [pl.BlockSpec(memory_space=pl.ANY)],
            out_specs=[pl.BlockSpec((width, part), lambda *_: (0, 0)), pl.BlockSpec((height - width, part), below)],
            input_output_aliases={} if out is None else {5: 1},
            cost_estimate=cost(12 * height * width * part, 8 * height * part),
            name=f"leaf_{i}",
        )(trailing, vth, vtl, ph, plo, extra)
        tops.append(top)
    for level in range(depth):
        for i in range(CHUNKS):
            far = swap(tops[i], "row", 1 << level)
            last = level == depth - 1
            at = functools.partial(lambda i, *_: (0, i), i)
            zero = lambda *_: (0, 0)
            result = pl.pallas_call(
                functools.partial(level_apply, width),
                grid=(1,),
                out_shape=whole if last else chunk,
                in_specs=[pl.BlockSpec((width, part), zero)] * 2
                + [pl.BlockSpec((width, 2 * width), zero)] * 2
                + [pl.BlockSpec(memory_space=pl.ANY)] * last,
                out_specs=pl.BlockSpec((width, part), at if last else zero),
                input_output_aliases={4: 0} if last else {},
                cost_estimate=cost(12 * width * width * part, 12 * width * part),
                name=f"level{level}_{i}",
            )(tops[i], far, *factors[level], *([out] * last))
            if last:
                out = result
            else:
                tops[i] = result
    return out


def solution(mesh):
    return jax.shard_map(
        per_device,
        mesh=mesh,
        in_specs=(
            P("row", "col"),
            P(("row", "col"), None),
            P(("row", "col"), None),
            P(("row", "col"), None),
            P(("row", "col"), None),
        ),
        out_specs=P("row", "col"),
        check_vma=False,
    )
```

```python
import functools

import jax
import jax.numpy as jnp
from jax import lax
from jax.experimental import pallas as pl
from jax.experimental.pallas import tpu as pltpu
from jax.sharding import PartitionSpec as P

CHUNKS = 8
STEP = 512
F32, BF16 = jnp.float32, jnp.bfloat16
VMEM = pl.BlockSpec(memory_space=pltpu.VMEM)
ANY = pl.BlockSpec(memory_space=pl.ANY)
TOKEN = pltpu.VMEM((8, 128), F32)


def call(kernel, name, args, outs, scratch=(), hbm_in=(), hbm_out=(), alias=None, after=()):
    count, waits = len(args), len(after)

    def body(*refs):
        kernel(*refs[:count], *refs[count + waits:])

    spaces = [pltpu.HBM if k in hbm_in else pltpu.VMEM for k in range(count)] + [pltpu.VMEM] * waits
    return pl.pallas_call(
        body,
        out_shape=[jax.ShapeDtypeStruct(o.shape, o.dtype) if k in hbm_out else o for k, o in enumerate(outs)],
        in_specs=[ANY if s is pltpu.HBM else VMEM for s in spaces],
        out_specs=[ANY if k in hbm_out else VMEM for k in range(len(outs))],
        scratch_shapes=list(scratch),
        input_output_aliases=alias or {},
        compiler_params=pltpu.CompilerParams(vmem_limit_bytes=20 << 20),
        cost_estimate=pl.CostEstimate(flops=1000, bytes_accessed=1000, transcendentals=0),
        name=name,
    )(*map(pltpu.with_memory_space_constraint, (*args, *after), spaces))


def swap(value, axis, mask):
    return lax.ppermute(value, axis, [(i, i ^ mask) for i in range(lax.axis_size(axis))])


def spread(piece, axis):
    n = lax.axis_size(axis)
    if n != 4:
        return [piece] + [swap(piece, axis, k) for k in range(1, n)]
    second = swap(piece, axis, 2)
    first = swap(piece, axis, 1)
    middle = lax.ppermute(piece, axis, [(1, 2), (2, 1)])
    ends = lax.ppermute(second, axis, [(1, 0), (2, 3)])
    return [piece, first, second, middle, ends]


def split(x):
    high = x.astype(BF16)
    return high, (x - high.astype(F32)).astype(BF16)


def dot3(ah, al, bh, bl, dims=((1,), (0,))):
    d = functools.partial(lax.dot_general, dimension_numbers=(dims, ((), ())), preferred_element_type=F32)
    return d(ah, bh) + (d(ah, bl) + d(al, bh))


def dotf(a, b, dims=((1,), (0,))):
    return dot3(*split(a), *split(b), dims)


def bit_of(level):
    return (lax.axis_index("row") >> level) & 1


def place(pieces, offset, rows, out):
    mine = lax.axis_index("col")

    def put(k, piece):
        to = pl.ds(pl.multiple_of((mine ^ k) * rows, rows), rows)
        out[to, :] = piece[pl.ds(offset, rows), :]

    whole = pieces if out.shape[0] == rows * len(pieces) else pieces[:-2]
    for k, piece in enumerate(whole):
        put(k, piece)
    if len(whole) < len(pieces):
        inner = (mine == 1) | (mine == 2)
        pl.when(inner)(lambda: put(3, pieces[-2]))
        pl.when(jnp.logical_not(inner))(lambda: put(3, pieces[-1]))


def pack(*refs):
    *sources, out, sems = refs
    copies, start = [], 0
    for k, source in enumerate(sources):
        copies.append(pltpu.make_async_copy(source, out.at[pl.ds(start, source.shape[0])], sems.at[k]))
        copies[-1].start()
        start += source.shape[0]
    for c in copies:
        c.wait()


def tree_blocks(n, start, rows, *refs):
    pieces, outs = refs[:n], refs[n:]
    for level, out in enumerate(outs):
        place(pieces, pl.multiple_of(start + bit_of(level) * rows, rows), rows, out)


def level_factors(level, own, far, fh, fl):
    width = own.shape[0]

    @pl.when(bit_of(level) == 0)
    def _():
        s, y = own[...], far[...]
        fh[:, :width], fl[:, :width] = split(s.T)
        fh[:, width:], fl[:, width:] = split(dotf(y, s).T)

    @pl.when(bit_of(level) == 1)
    def _():
        y, s = own[...], far[...]
        ys = dotf(y, s, ((1,), (1,)))
        fh[:, width:], fl[:, width:] = split(ys)
        fh[:, :width], fl[:, :width] = split(dotf(ys, y, ((1,), (1,))))


def load(c, out, high, low, buffer, sems):
    size = buffer.shape[2]
    copies = []
    for k in range(buffer.shape[0]):
        copies.append(pltpu.make_async_copy(c.at[:, pl.ds(k * size, size)], buffer.at[k], sems.at[k]))
        copies[-1].start()
    for k, copy in enumerate(copies):
        at = pl.ds(k * size, size)
        copy.wait()
        out[:, at] = buffer[k]
        high[:, at], low[:, at] = split(buffer[k])


def leaf_factors(n, vr, tr, *refs):
    pieces, (vth, vtl, ph, plo), (v, t) = refs[:n], refs[n:n + 4], refs[n + 4:]
    place(pieces, 0, vr, v)
    place(pieces, vr, tr, t)
    full = v[...]
    vth[...], vtl[...] = split(full.T)
    ph[...], plo[...] = split(dotf(full, t[...], ((1,), (1,))))


def leaf_apply(start, c, ch, cl, vth, vtl, ph, plo, top, *outs):
    width, size = top.shape
    at = pl.ds(start, size)
    h, l = split(dot3(vth[...], vtl[...], ch[:, at], cl[:, at]))
    if len(outs) == 2:
        outs[0][...], outs[1][...] = h, l
        top[...] = c[:width, at] - dot3(ph[:width, :], plo[:width, :], h, l)
    else:
        change = dot3(ph[...], plo[...], h, l)
        top[...] = c[:width, at] - change[:width]
        outs[0][...] = c[width:, at] - change[width:]


def rest_apply(start, c, ph, plo, ih, il, out):
    width, size = ih.shape
    out[...] = c[width:, pl.ds(start, size)] - dot3(ph[width:, :], plo[width:, :], ih[...], il[...])


def level_result(start, own, far, fh, fl, size):
    width = own.shape[0]
    mine, other = own[:, pl.ds(start, size)], far[:, pl.ds(start, size)]
    change = dot3(fh[:, :width], fl[:, :width], *split(mine)) + dot3(fh[:, width:], fl[:, width:], *split(other))
    return mine - change


def level_apply(start, own, far, fh, fl, out):
    out[...] = level_result(start, own, far, fh, fl, out.shape[1])


def store(sources, out, top, sems):
    copies = []
    for k, source in enumerate(sources):
        rows, size = source.shape
        to = out.at[pl.ds(top, rows), pl.ds(k * size, size)]
        copies.append(pltpu.make_async_copy(source, to, sems.at[k]))
        copies[-1].start()
    return copies


def lower_store(*refs):
    *sources, out, sems = refs
    for copy in store(sources, out, out.shape[0] - sources[0].shape[0], sems):
        copy.wait()


def last_apply(own, far, fh, fl, *refs):
    *sources, _, out, buffer, sems = refs
    copies = store(sources, out, 0, sems)
    width, size = own.shape
    buffer[...] = level_result(0, own, far, fh, fl, size)
    to = out.at[pl.ds(0, width), pl.ds(len(sources) * size, size)]
    copies.append(pltpu.make_async_copy(buffer, to, sems.at[len(sources)]))
    copies[-1].start()
    for copy in copies:
        copy.wait()


def per_device(trailing, leaf_v, leaf_t, tree_y, tree_t):
    height, columns = trailing.shape
    width = leaf_v.shape[1]
    vr, tr = leaf_v.shape[0], leaf_t.shape[0]
    depth = lax.axis_size("row").bit_length() - 1
    part = columns // CHUNKS
    steps = columns // STEP
    block, block16 = pltpu.VMEM((width, width), F32), lambda *shape: pltpu.VMEM(shape, BF16)

    (packed,) = call(
        pack,
        "pack",
        (leaf_v, leaf_t, tree_t, tree_y),
        [pltpu.VMEM((vr + 3 * tr, width), F32)],
        [pltpu.SemaphoreType.DMA((4,))],
        hbm_in=range(4),
    )
    pieces = spread(packed, "col")
    c, ch, cl = call(
        load,
        "load",
        (trailing,),
        [pltpu.VMEM((height, columns), F32)] + [block16(height, columns)] * 2,
        [pltpu.VMEM((steps, height, STEP), F32), pltpu.SemaphoreType.DMA((steps,))],
        hbm_in=(0,),
        after=pieces[2:3],
    )
    owns = call(functools.partial(tree_blocks, len(pieces), vr + tr, tr), "tree_blocks", pieces, [block] * depth, after=[ch])
    factors = [
        call(
            functools.partial(level_factors, level),
            f"factors{level}",
            (owns[level], swap(owns[level], "row", 1 << level)),
            [block16(width, 2 * width)] * 2,
        )
        for level in range(depth)
    ]
    vth, vtl, ph, plo = call(
        functools.partial(leaf_factors, len(pieces), vr, tr),
        "leaf_factors",
        pieces,
        [block16(width, height)] * 2 + [block16(height, width)] * 2,
        [pltpu.VMEM((height, width), F32), block],
    )

    made = [[] for _ in range(depth - 1)]
    sent = [[] for _ in range(depth - 1)]
    pending = {}

    def advance(level, own, far, at, waits):
        (chunk,) = call(
            functools.partial(level_apply, at),
            f"level{level}",
            (own, far, *factors[level]),
            [pltpu.VMEM((width, part), F32)],
            after=waits,
        )
        made[level].append(chunk)
        sent[level].append(swap(chunk, "row", 2 << level))

    def later(k):
        for level in range(1, depth - 1):
            waits = [made[0][1]] if level == 1 and k == 0 else []
            if level == 1 and k == 1:
                waits = [factors[-1][0]]
            if level == depth - 2 and k >= 2:
                waits = done[k - 2:k - 1]
            advance(level, made[level - 1][k], sent[level - 1][k], 0, waits)

    done, rests, tops, fars = [], [], [], []

    def leaf(k):
        above, below = pltpu.VMEM((width, part), F32), pltpu.VMEM((height - width, part), F32)
        top, *others = call(
            functools.partial(leaf_apply, k * part),
            f"leaf_{k}",
            (c, ch, cl, vth, vtl, ph, plo),
            [above] + ([block16(width, part)] * 2 if k < 2 else [below]),
            after=tops if k == 1 else made[0][k - 2:k - 1] if k else (),
        )
        if k < 2:
            others = call(
                functools.partial(rest_apply, k * part), f"rest_{k}", (c, ph, plo, *others), [below], after=made[0][k:k + 1]
            )
        rests.extend(others)
        tops.append(top)
        fars.append(swap(top, "row", 1))

    def first_level(k):
        waits = made[min(1, depth - 2)][k - 2:k - 1] if k >= 2 else [factors[1][0]] * k
        advance(0, tops[k], fars[k], 0, waits)

    leaf(0)
    leaf(1)
    first_level(0)
    first_level(1)
    leaf(2)
    for k in range(CHUNKS):
        later(k)
        if k + 2 < CHUNKS:
            first_level(k + 2)
        if k + 3 < CHUNKS:
            leaf(k + 3)
        if k < CHUNKS - 1:
            done += call(
                functools.partial(level_apply, 0),
                "last",
                (made[-1][k], sent[-1][k], *factors[-1]),
                [pltpu.VMEM((width, part), F32)],
            )
    whole = jax.ShapeDtypeStruct((height, columns), F32)
    sems = pltpu.SemaphoreType.DMA((CHUNKS,))
    (out,) = call(lower_store, "lower_store", rests, [whole], [sems], hbm_out=(0,))
    (out,) = call(
        last_apply,
        "finish",
        (made[-1][-1], sent[-1][-1], *factors[-1], *done, out),
        [whole],
        [pltpu.VMEM((width, part), F32), sems],
        hbm_in=(3 + CHUNKS,),
        hbm_out=(0,),
        alias={3 + CHUNKS: 0},
    )
    return out


def solution(mesh):
    return jax.shard_map(
        per_device,
        mesh=mesh,
        in_specs=(
            P("row", "col"),
            P(("row", "col"), None),
            P(("row", "col"), None),
            P(("row", "col"), None),
            P(("row", "col"), None),
        ),
        out_specs=P("row", "col"),
        check_vma=False,
    )
```

```python
import functools

import jax
import jax.numpy as jnp
from jax import lax
from jax.experimental import pallas as pl
from jax.experimental.pallas import tpu as pltpu
from jax.sharding import PartitionSpec as P

CHUNKS = 8
STEP = 512
F32, BF16 = jnp.float32, jnp.bfloat16
VMEM = pl.BlockSpec(memory_space=pltpu.VMEM)
ANY = pl.BlockSpec(memory_space=pl.ANY)
TOKEN = pltpu.VMEM((8, 128), F32)


def call(kernel, name, args, outs, scratch=(), hbm_in=(), hbm_out=(), alias=None, after=()):
    count, waits = len(args), len(after)

    def body(*refs):
        kernel(*refs[:count], *refs[count + waits:])

    spaces = [pltpu.HBM if k in hbm_in else pltpu.VMEM for k in range(count)] + [pltpu.VMEM] * waits
    return pl.pallas_call(
        body,
        out_shape=[jax.ShapeDtypeStruct(o.shape, o.dtype) if k in hbm_out else o for k, o in enumerate(outs)],
        in_specs=[ANY if s is pltpu.HBM else VMEM for s in spaces],
        out_specs=[ANY if k in hbm_out else VMEM for k in range(len(outs))],
        scratch_shapes=list(scratch),
        input_output_aliases=alias or {},
        compiler_params=pltpu.CompilerParams(vmem_limit_bytes=20 << 20),
        cost_estimate=pl.CostEstimate(flops=1000, bytes_accessed=1000, transcendentals=0),
        name=name,
    )(*map(pltpu.with_memory_space_constraint, (*args, *after), spaces))


def swap(value, axis, mask):
    return lax.ppermute(value, axis, [(i, i ^ mask) for i in range(lax.axis_size(axis))])


def spread(whole, halves, axis):
    n = lax.axis_size(axis)
    if n != 4:
        return [whole] + [swap(whole, axis, k) for k in range(1, n)]
    seconds = [swap(half, axis, 2) for half in halves]
    first = swap(whole, axis, 1)
    middle = lax.ppermute(whole, axis, [(1, 2), (2, 1)])
    ends = [lax.ppermute(second, axis, [(1, 0), (2, 3)]) for second in seconds]
    return [whole, first, middle, *seconds, *ends]


def split(x):
    high = x.astype(BF16)
    return high, (x - high.astype(F32)).astype(BF16)


def dot3(ah, al, bh, bl, dims=((1,), (0,))):
    d = functools.partial(lax.dot_general, dimension_numbers=(dims, ((), ())), preferred_element_type=F32)
    return d(ah, bh) + (d(ah, bl) + d(al, bh))


def dotf(a, b, dims=((1,), (0,))):
    return dot3(*split(a), *split(b), dims)


def bit_of(level):
    return (lax.axis_index("row") >> level) & 1


def place(pieces, start, rows, out):
    mine = lax.axis_index("col")
    span = pl.ds(start, rows)

    def put(k, *parts):
        to = pl.ds(pl.multiple_of((mine ^ k) * rows, rows), rows)
        size = out.shape[1] // len(parts)
        for i, part in enumerate(parts):
            out[to, pl.ds(i * size, size)] = part[span, :]

    if out.shape[0] == rows * len(pieces):
        for k, piece in enumerate(pieces):
            put(k, piece)
        return
    put(0, pieces[0])
    put(1, pieces[1])
    put(2, *pieces[3:5])
    inner = (mine == 1) | (mine == 2)
    pl.when(inner)(lambda: put(3, pieces[2]))
    pl.when(jnp.logical_not(inner))(lambda: put(3, *pieces[5:7]))


def pack(*refs):
    *sources, whole, left, right, sems = refs
    size = left.shape[1]
    copies, start = [], 0
    for source in sources:
        to = pl.ds(start, source.shape[0])
        for half, target in ((pl.ds(0, 2 * size), whole), (pl.ds(0, size), left), (pl.ds(size, size), right)):
            copies.append(pltpu.make_async_copy(source.at[:, half], target.at[to], sems.at[len(copies)]))
            copies[-1].start()
        start += source.shape[0]
    for c in copies:
        c.wait()


def tree_blocks(n, start, rows, *refs):
    pieces, outs = refs[:n], refs[n:]
    for level, out in enumerate(outs):
        place(pieces, pl.multiple_of(start + bit_of(level) * rows, rows), rows, out)


def level_factors(level, own, far, fh, fl):
    width = own.shape[0]

    @pl.when(bit_of(level) == 0)
    def _():
        s, y = own[...], far[...]
        fh[:, :width], fl[:, :width] = split(s.T)
        fh[:, width:], fl[:, width:] = split(dotf(y, s).T)

    @pl.when(bit_of(level) == 1)
    def _():
        y, s = own[...], far[...]
        ys = dotf(y, s, ((1,), (1,)))
        fh[:, width:], fl[:, width:] = split(ys)
        fh[:, :width], fl[:, :width] = split(dotf(ys, y, ((1,), (1,))))


def load(c, out, high, low, buffer, sems):
    size = buffer.shape[2]
    copies = []
    for k in range(buffer.shape[0]):
        copies.append(pltpu.make_async_copy(c.at[:, pl.ds(k * size, size)], buffer.at[k], sems.at[k]))
        copies[-1].start()
    for k, copy in enumerate(copies):
        at = pl.ds(k * size, size)
        copy.wait()
        out[:, at] = buffer[k]
        high[:, at], low[:, at] = split(buffer[k])


def leaf_factors(n, vr, tr, *refs):
    pieces, (vth, vtl, ph, plo), (v, t) = refs[:n], refs[n:n + 4], refs[n + 4:]
    place(pieces, 0, vr, v)
    place(pieces, vr, tr, t)
    full = v[...]
    vth[...], vtl[...] = split(full.T)
    ph[...], plo[...] = split(dotf(full, t[...], ((1,), (1,))))


def leaf_apply(start, c, ch, cl, vth, vtl, ph, plo, top, *outs):
    width, size = top.shape
    at = pl.ds(start, size)
    h, l = split(dot3(vth[...], vtl[...], ch[:, at], cl[:, at]))
    if len(outs) == 2:
        outs[0][...], outs[1][...] = h, l
        top[...] = c[:width, at] - dot3(ph[:width, :], plo[:width, :], h, l)
    else:
        change = dot3(ph[...], plo[...], h, l)
        top[...] = c[:width, at] - change[:width]
        outs[0][...] = c[width:, at] - change[width:]


def rest_apply(start, c, ph, plo, ih, il, out):
    width, size = ih.shape
    out[...] = c[width:, pl.ds(start, size)] - dot3(ph[width:, :], plo[width:, :], ih[...], il[...])


def level_result(start, own, far, fh, fl, size):
    width = own.shape[0]
    mine, other = own[:, pl.ds(start, size)], far[:, pl.ds(start, size)]
    change = dot3(fh[:, :width], fl[:, :width], *split(mine)) + dot3(fh[:, width:], fl[:, width:], *split(other))
    return mine - change


def level_apply(start, own, far, fh, fl, out):
    out[...] = level_result(start, own, far, fh, fl, out.shape[1])


def store(sources, out, top, sems):
    copies = []
    for k, source in enumerate(sources):
        rows, size = source.shape
        to = out.at[pl.ds(top, rows), pl.ds(k * size, size)]
        copies.append(pltpu.make_async_copy(source, to, sems.at[k]))
        copies[-1].start()
    return copies


def lower_store(*refs):
    *sources, out, sems = refs
    for copy in store(sources, out, out.shape[0] - sources[0].shape[0], sems):
        copy.wait()


def last_apply(own, far, fh, fl, *refs):
    *sources, _, out, buffer, sems = refs
    copies = store(sources, out, 0, sems)
    width, size = own.shape
    buffer[...] = level_result(0, own, far, fh, fl, size)
    to = out.at[pl.ds(0, width), pl.ds(len(sources) * size, size)]
    copies.append(pltpu.make_async_copy(buffer, to, sems.at[len(sources)]))
    copies[-1].start()
    for copy in copies:
        copy.wait()


def per_device(trailing, leaf_v, leaf_t, tree_y, tree_t):
    height, columns = trailing.shape
    width = leaf_v.shape[1]
    vr, tr = leaf_v.shape[0], leaf_t.shape[0]
    depth = lax.axis_size("row").bit_length() - 1
    part = columns // CHUNKS
    steps = columns // STEP
    block, block16 = pltpu.VMEM((width, width), F32), lambda *shape: pltpu.VMEM(shape, BF16)

    rows = vr + 3 * tr
    whole, *halves = call(
        pack,
        "pack",
        (leaf_v, leaf_t, tree_t, tree_y),
        [pltpu.VMEM((rows, width), F32)] + [pltpu.VMEM((rows, width // 2), F32)] * 2,
        [pltpu.SemaphoreType.DMA((12,))],
        hbm_in=range(4),
    )
    pieces = spread(whole, halves, "col")
    c, ch, cl = call(
        load,
        "load",
        (trailing,),
        [pltpu.VMEM((height, columns), F32)] + [block16(height, columns)] * 2,
        [pltpu.VMEM((steps, height, STEP), F32), pltpu.SemaphoreType.DMA((steps,))],
        hbm_in=(0,),
        after=pieces[3:5],
    )
    owns = call(functools.partial(tree_blocks, len(pieces), vr + tr, tr), "tree_blocks", pieces, [block] * depth, after=[ch])
    factors = [
        call(
            functools.partial(level_factors, level),
            f"factors{level}",
            (owns[level], swap(owns[level], "row", 1 << level)),
            [block16(width, 2 * width)] * 2,
        )
        for level in range(depth)
    ]
    vth, vtl, ph, plo = call(
        functools.partial(leaf_factors, len(pieces), vr, tr),
        "leaf_factors",
        pieces,
        [block16(width, height)] * 2 + [block16(height, width)] * 2,
        [pltpu.VMEM((height, width), F32), block],
    )

    made = [[] for _ in range(depth - 1)]
    sent = [[] for _ in range(depth - 1)]
    pending = {}

    def advance(level, own, far, at, waits):
        (chunk,) = call(
            functools.partial(level_apply, at),
            f"level{level}",
            (own, far, *factors[level]),
            [pltpu.VMEM((width, part), F32)],
            after=waits,
        )
        made[level].append(chunk)
        sent[level].append(swap(chunk, "row", 2 << level))

    def later(k):
        for level in range(1, depth - 1):
            waits = [made[0][1]] if level == 1 and k == 0 else []
            if level == 1 and k == 1:
                waits = [factors[-1][0]]
            if level == depth - 2 and k >= 2:
                waits = done[k - 2:k - 1]
            advance(level, made[level - 1][k], sent[level - 1][k], 0, waits)

    done, rests, tops, fars = [], [], [], []

    def make_leaf(k):
        above, below = pltpu.VMEM((width, part), F32), pltpu.VMEM((height - width, part), F32)
        top, *others = call(
            functools.partial(leaf_apply, k * part),
            f"leaf_{k}",
            (c, ch, cl, vth, vtl, ph, plo),
            [above] + ([block16(width, part)] * 2 if k < 2 else [below]),
            after=tops if k == 1 else made[0][k - 2:k - 1] if k else (),
        )
        if k < 2:
            others = call(
                functools.partial(rest_apply, k * part), f"rest_{k}", (c, ph, plo, *others), [below], after=made[0][k:k + 1]
            )
        rests.extend(others)
        tops.append(top)
        fars.append(swap(top, "row", 1))

    def first_level(k):
        waits = made[min(1, depth - 2)][k - 2:k - 1] if k >= 2 else [factors[1][0]] * k
        advance(0, tops[k], fars[k], 0, waits)

    make_leaf(0)
    make_leaf(1)
    first_level(0)
    first_level(1)
    make_leaf(2)
    for k in range(CHUNKS):
        later(k)
        if k + 2 < CHUNKS:
            first_level(k + 2)
        if k + 3 < CHUNKS:
            make_leaf(k + 3)
        if k < CHUNKS - 1:
            done += call(
                functools.partial(level_apply, 0),
                "last",
                (made[-1][k], sent[-1][k], *factors[-1]),
                [pltpu.VMEM((width, part), F32)],
            )
    whole = jax.ShapeDtypeStruct((height, columns), F32)
    sems = pltpu.SemaphoreType.DMA((CHUNKS,))
    (out,) = call(lower_store, "lower_store", rests, [whole], [sems], hbm_out=(0,))
    (out,) = call(
        last_apply,
        "finish",
        (made[-1][-1], sent[-1][-1], *factors[-1], *done, out),
        [whole],
        [pltpu.VMEM((width, part), F32), sems],
        hbm_in=(3 + CHUNKS,),
        hbm_out=(0,),
        alias={3 + CHUNKS: 0},
    )
    return out


def solution(mesh):
    return jax.shard_map(
        per_device,
        mesh=mesh,
        in_specs=(
            P("row", "col"),
            P(("row", "col"), None),
            P(("row", "col"), None),
            P(("row", "col"), None),
            P(("row", "col"), None),
        ),
        out_specs=P("row", "col"),
        check_vma=False,
    )
```

```python
import functools

import jax
import jax.numpy as jnp
from jax import lax
from jax.experimental import pallas as pl
from jax.experimental.pallas import tpu as pltpu
from jax.sharding import PartitionSpec as P

CHUNKS = 8
LEAVES = {2: (2, 4), 3: (3, 5)}
STEP = 512
F32, BF16 = jnp.float32, jnp.bfloat16
VMEM = pl.BlockSpec(memory_space=pltpu.VMEM)
ANY = pl.BlockSpec(memory_space=pl.ANY)
TOKEN = pltpu.VMEM((8, 128), F32)


def call(kernel, name, args, outs, scratch=(), hbm_in=(), hbm_out=(), alias=None, after=(), size=1000):
    count, waits = len(args), len(after)

    def body(*refs):
        kernel(*refs[:count], *refs[count + waits:])

    spaces = [pltpu.HBM if k in hbm_in else pltpu.VMEM for k in range(count)] + [pltpu.VMEM] * waits
    return pl.pallas_call(
        body,
        out_shape=[jax.ShapeDtypeStruct(o.shape, o.dtype) if k in hbm_out else o for k, o in enumerate(outs)],
        in_specs=[ANY if s is pltpu.HBM else VMEM for s in spaces],
        out_specs=[ANY if k in hbm_out else VMEM for k in range(len(outs))],
        scratch_shapes=list(scratch),
        input_output_aliases=alias or {},
        compiler_params=pltpu.CompilerParams(vmem_limit_bytes=20 << 20),
        cost_estimate=pl.CostEstimate(flops=size, bytes_accessed=1000, transcendentals=0),
        name=name,
    )(*map(pltpu.with_memory_space_constraint, (*args, *after), spaces))


def swap(value, axis, mask):
    return lax.ppermute(value, axis, [(i, i ^ mask) for i in range(lax.axis_size(axis))])


def spread(whole, halves, axis):
    n = lax.axis_size(axis)
    if n != 4:
        return [whole] + [swap(whole, axis, k) for k in range(1, n)]
    seconds = [swap(half, axis, 2) for half in halves]
    first = swap(whole, axis, 1)
    middle = lax.ppermute(whole, axis, [(1, 2), (2, 1)])
    ends = [lax.ppermute(second, axis, [(1, 0), (2, 3)]) for second in seconds]
    return [whole, first, middle, *seconds, *ends]


def split(x):
    high = x.astype(BF16)
    return high, (x - high.astype(F32)).astype(BF16)


def dot3(ah, al, bh, bl, dims=((1,), (0,))):
    d = functools.partial(lax.dot_general, dimension_numbers=(dims, ((), ())), preferred_element_type=F32)
    return d(ah, bh) + (d(ah, bl) + d(al, bh))


def dotf(a, b, dims=((1,), (0,))):
    return dot3(*split(a), *split(b), dims)


def bit_of(level):
    return (lax.axis_index("row") >> level) & 1


def place(pieces, start, rows, out):
    mine = lax.axis_index("col")
    span = pl.ds(start, rows)

    def put(k, *parts):
        to = pl.ds(pl.multiple_of((mine ^ k) * rows, rows), rows)
        size = out.shape[1] // len(parts)
        for i, part in enumerate(parts):
            out[to, pl.ds(i * size, size)] = part[span, :]

    if out.shape[0] == rows * len(pieces):
        for k, piece in enumerate(pieces):
            put(k, piece)
        return
    put(0, pieces[0])
    put(1, pieces[1])
    put(2, *pieces[3:5])
    inner = (mine == 1) | (mine == 2)
    pl.when(inner)(lambda: put(3, pieces[2]))
    pl.when(jnp.logical_not(inner))(lambda: put(3, *pieces[5:7]))


def pack(*refs):
    *sources, whole, left, right, sems = refs
    size = left.shape[1]
    copies, start = [], 0
    for source in sources:
        to = pl.ds(start, source.shape[0])
        for half, target in ((pl.ds(0, 2 * size), whole), (pl.ds(0, size), left), (pl.ds(size, size), right)):
            copies.append(pltpu.make_async_copy(source.at[:, half], target.at[to], sems.at[len(copies)]))
            copies[-1].start()
        start += source.shape[0]
    for c in copies:
        c.wait()


def tree_blocks(n, start, rows, *refs):
    pieces, outs, odd = refs[:n], refs[n:-1], refs[-1]
    for level, out in enumerate(outs):
        place(pieces, pl.multiple_of(start + bit_of(level) * rows, rows), rows, out)
    mine = lax.axis_index("col")
    for k in range(odd.shape[0] // rows):
        odd[pl.ds(k * rows, rows), :] = outs[1][pl.ds(pl.multiple_of((mine ^ (2 * k + 1)) * rows, rows), rows), :]


def even_rows(n, start, rows, *refs):
    span = pl.ds(pl.multiple_of(start + bit_of(1) * rows, rows), rows)
    out = refs[-1]
    if n == 4:
        whole, left, right = refs[:-1]
        size = left.shape[1]
        out[:rows, :] = whole[span, :]
        out[rows:, :size], out[rows:, size:] = left[span, :], right[span, :]
    else:
        for k, piece in enumerate(refs[:-1]):
            out[pl.ds(k * rows, rows), :] = piece[span, :]


def level_factors(level, rows, own, *refs):
    width = own.shape[0]
    if len(refs) == 3:
        far, fh, fl = refs
    else:
        even, odd, fh, fl, far = refs
        mine = lax.axis_index("col")
        for k in range(width // rows):
            to = pl.ds(pl.multiple_of((mine ^ k) * rows, rows), rows)
            far[to, :] = (odd if k % 2 else even)[pl.ds(k // 2 * rows, rows), :]

    @pl.when(bit_of(level) == 0)
    def _():
        s, y = own[...], far[...]
        fh[:, :width], fl[:, :width] = split(s.T)
        fh[:, width:], fl[:, width:] = split(dotf(y, s).T)

    @pl.when(bit_of(level) == 1)
    def _():
        y, s = own[...], far[...]
        ys = dotf(y, s, ((1,), (1,)))
        fh[:, width:], fl[:, width:] = split(ys)
        fh[:, :width], fl[:, :width] = split(dotf(ys, y, ((1,), (1,))))


def load(c, out, high, low, buffer, sems):
    size = buffer.shape[2]
    copies = []
    for k in range(buffer.shape[0]):
        copies.append(pltpu.make_async_copy(c.at[:, pl.ds(k * size, size)], buffer.at[k], sems.at[k]))
        copies[-1].start()
    for k, copy in enumerate(copies):
        at = pl.ds(k * size, size)
        copy.wait()
        out[:, at] = buffer[k]
        high[:, at], low[:, at] = split(buffer[k])


def leaf_factors(n, vr, tr, *refs):
    pieces, (vth, vtl, ph, plo), (v, t) = refs[:n], refs[n:n + 4], refs[n + 4:]
    place(pieces, 0, vr, v)
    place(pieces, vr, tr, t)
    full = v[...]
    vth[...], vtl[...] = split(full.T)
    ph[...], plo[...] = split(dotf(full, t[...], ((1,), (1,))))


def leaf_apply(starts, c, ch, cl, vth, vtl, ph, plo, *outs):
    for k, start in enumerate(starts):
        top, *others = outs[k * len(outs) // len(starts):(k + 1) * len(outs) // len(starts)]
        width, size = top.shape
        at = pl.ds(start, size)
        h, l = split(dot3(vth[...], vtl[...], ch[:, at], cl[:, at]))
        if len(others) == 2:
            others[0][...], others[1][...] = h, l
            top[...] = c[:width, at] - dot3(ph[:width, :], plo[:width, :], h, l)
        else:
            change = dot3(ph[...], plo[...], h, l)
            top[...] = c[:width, at] - change[:width]
            others[0][...] = c[width:, at] - change[width:]


def rest_apply(start, c, ph, plo, ih, il, out):
    width, size = ih.shape
    out[...] = c[width:, pl.ds(start, size)] - dot3(ph[width:, :], plo[width:, :], ih[...], il[...])


def level_result(start, own, far, fh, fl, size):
    width = own.shape[0]
    mine, other = own[:, pl.ds(start, size)], far[:, pl.ds(start, size)]
    change = dot3(fh[:, :width], fl[:, :width], *split(mine)) + dot3(fh[:, width:], fl[:, width:], *split(other))
    return mine - change


def level_apply(start, own, far, fh, fl, out):
    out[...] = level_result(start, own, far, fh, fl, out.shape[1])


def store(sources, out, top, left, sems, first=0):
    copies = []
    for k, source in enumerate(sources):
        rows, size = source.shape
        to = out.at[pl.ds(top, rows), pl.ds(left + k * size, size)]
        copies.append(pltpu.make_async_copy(source, to, sems.at[first + k]))
        copies[-1].start()
    return copies


def early_store(*refs):
    *sources, out, sems = refs
    lower, upper = sources[:CHUNKS], sources[CHUNKS:]
    for copy in store(lower, out, out.shape[0] - lower[0].shape[0], 0, sems) + store(upper, out, 0, 0, sems, CHUNKS):
        copy.wait()


def last_apply(own, far, fh, fl, *refs):
    *sources, _, out, buffer, sems = refs
    width, size = own.shape
    copies = store(sources, out, 0, out.shape[1] - (len(sources) + 1) * size, sems)
    buffer[...] = level_result(0, own, far, fh, fl, size)
    to = out.at[pl.ds(0, width), pl.ds(out.shape[1] - size, size)]
    copies.append(pltpu.make_async_copy(buffer, to, sems.at[len(sources)]))
    copies[-1].start()
    for copy in copies:
        copy.wait()


def per_device(trailing, leaf_v, leaf_t, tree_y, tree_t):
    height, columns = trailing.shape
    width = leaf_v.shape[1]
    vr, tr = leaf_v.shape[0], leaf_t.shape[0]
    depth = lax.axis_size("row").bit_length() - 1
    part = columns // CHUNKS
    steps = columns // STEP
    block, block16 = pltpu.VMEM((width, width), F32), lambda *shape: pltpu.VMEM(shape, BF16)

    rows = vr + 3 * tr
    whole, *halves = call(
        pack,
        "pack",
        (leaf_v, leaf_t, tree_t, tree_y),
        [pltpu.VMEM((rows, width), F32)] + [pltpu.VMEM((rows, width // 2), F32)] * 2,
        [pltpu.SemaphoreType.DMA((12,))],
        hbm_in=range(4),
    )
    pieces = spread(whole, halves, "col")
    n = lax.axis_size("col")
    some = [pieces[0], *pieces[3:5]] if n == 4 else pieces[0::2]
    half = pltpu.VMEM((width // 2, width), F32)
    (even,) = call(functools.partial(even_rows, n, vr + tr, tr), "even_rows", some, [half])
    even = swap(even, "row", 2)
    c, ch, cl = call(
        load,
        "load",
        (trailing,),
        [pltpu.VMEM((height, columns), F32)] + [block16(height, columns)] * 2,
        [pltpu.VMEM((steps, height, STEP), F32), pltpu.SemaphoreType.DMA((steps,))],
        hbm_in=(0,),
        after=pieces[3:5],
    )
    *owns, odd = call(
        functools.partial(tree_blocks, len(pieces), vr + tr, tr), "tree_blocks", pieces, [block] * depth + [half], after=[ch]
    )
    odd = swap(odd, "row", 2)
    factors = [
        call(
            functools.partial(level_factors, level, tr),
            f"factors{level}",
            (owns[level], *([even, odd] if level == 1 else [swap(owns[level], "row", 1 << level)])),
            [block16(width, 2 * width)] * 2,
            [block] * (level == 1),
            size=2 * 10**9 if level == 1 else 1000,
        )
        for level in range(depth)
    ]
    vth, vtl, ph, plo = call(
        functools.partial(leaf_factors, len(pieces), vr, tr),
        "leaf_factors",
        pieces,
        [block16(width, height)] * 2 + [block16(height, width)] * 2,
        [pltpu.VMEM((height, width), F32), block],
        after=[even],
    )

    made = [[] for _ in range(depth - 1)]
    sent = [[] for _ in range(depth - 1)]
    pending = {}

    def advance(level, own, far, at, waits):
        (chunk,) = call(
            functools.partial(level_apply, at),
            f"level{level}",
            (own, far, *factors[level]),
            [pltpu.VMEM((width, part), F32)],
            after=waits,
        )
        made[level].append(chunk)
        sent[level].append(swap(chunk, "row", 2 << level))

    def later(k):
        for level in range(1, depth - 1):
            waits = [made[0][1]] if level == 1 and k == 0 else []
            if level == 1 and k == 1:
                waits = [factors[-1][0]]
            if level == depth - 2 and k >= 2:
                waits = done[k - 2:k - 1]
            advance(level, made[level - 1][k], sent[level - 1][k], 0, waits)

    done, rests, tops, fars = [], {}, {}, {}

    def make_leaf(k):
        if k in tops:
            return
        above, below = pltpu.VMEM((width, part), F32), pltpu.VMEM((height - width, part), F32)
        ks = LEAVES.get(k, (k,))
        outs = call(
            functools.partial(leaf_apply, [j * part for j in ks]),
            f"leaf_{k}",
            (c, ch, cl, vth, vtl, ph, plo),
            [above, *([block16(width, part)] * 2 if k < 2 else [below])] * len(ks),
            after=[tops[0]] if k == 1 else made[0][k - 2:k - 1] if k else (),
        )
        if k < 2:
            outs = (outs[0], *call(
                functools.partial(rest_apply, k * part), f"rest_{k}", (c, ph, plo, *outs[1:]), [below], after=made[0][k:k + 1]
            ))
        for j, top, rest in zip(ks, outs[0::2], outs[1::2]):
            tops[j], rests[j], fars[j] = top, rest, swap(top, "row", 1)

    def first_level(k):
        waits = made[min(1, depth - 2)][k - 2:k - 1] if k >= 2 else [factors[1][0]]
        advance(0, tops[k], fars[k], 0, waits)

    make_leaf(0)
    make_leaf(1)
    first_level(0)
    first_level(1)
    make_leaf(2)
    for k in range(CHUNKS):
        later(k)
        if k + 2 < CHUNKS:
            first_level(k + 2)
        if k + 3 < CHUNKS:
            make_leaf(k + 3)
        if k < CHUNKS - 1:
            done += call(
                functools.partial(level_apply, 0),
                "last",
                (made[-1][k], sent[-1][k], *factors[-1]),
                [pltpu.VMEM((width, part), F32)],
            )
    whole = jax.ShapeDtypeStruct((height, columns), F32)
    sems, kept = pltpu.SemaphoreType.DMA((2 * CHUNKS,)), CHUNKS - 3
    early = [rests[k] for k in range(CHUNKS)] + done[:kept]
    (out,) = call(early_store, "early_store", early, [whole], [sems], hbm_out=(0,))
    late = done[kept:]
    (out,) = call(
        last_apply,
        "finish",
        (made[-1][-1], sent[-1][-1], *factors[-1], *late, out),
        [whole],
        [pltpu.VMEM((width, part), F32), sems],
        hbm_in=(4 + len(late),),
        hbm_out=(0,),
        alias={4 + len(late): 0},
    )
    return out


def solution(mesh):
    return jax.shard_map(
        per_device,
        mesh=mesh,
        in_specs=(
            P("row", "col"),
            P(("row", "col"), None),
            P(("row", "col"), None),
            P(("row", "col"), None),
            P(("row", "col"), None),
        ),
        out_specs=P("row", "col"),
        check_vma=False,
    )
```

```python
import functools

import jax
import jax.numpy as jnp
from jax import lax
from jax.experimental import pallas as pl
from jax.experimental.pallas import tpu as pltpu
from jax.sharding import PartitionSpec as P

CHUNKS = 8
LEAVES = {2: (2, 4), 3: (3, 5)}
STEP = 512
F32, BF16 = jnp.float32, jnp.bfloat16
VMEM = pl.BlockSpec(memory_space=pltpu.VMEM)
ANY = pl.BlockSpec(memory_space=pl.ANY)
TOKEN = pltpu.VMEM((8, 128), F32)


def call(kernel, name, args, outs, scratch=(), hbm_in=(), hbm_out=(), alias=None, after=(), size=1000):
    count, waits = len(args), len(after)

    def body(*refs):
        kernel(*refs[:count], *refs[count + waits:])

    spaces = [pltpu.HBM if k in hbm_in else pltpu.VMEM for k in range(count)] + [pltpu.VMEM] * waits
    return pl.pallas_call(
        body,
        out_shape=[jax.ShapeDtypeStruct(o.shape, o.dtype) if k in hbm_out else o for k, o in enumerate(outs)],
        in_specs=[ANY if s is pltpu.HBM else VMEM for s in spaces],
        out_specs=[ANY if k in hbm_out else VMEM for k in range(len(outs))],
        scratch_shapes=list(scratch),
        input_output_aliases=alias or {},
        compiler_params=pltpu.CompilerParams(vmem_limit_bytes=20 << 20),
        cost_estimate=pl.CostEstimate(flops=size, bytes_accessed=1000, transcendentals=0),
        name=name,
    )(*map(pltpu.with_memory_space_constraint, (*args, *after), spaces))


def swap(value, axis, mask):
    return lax.ppermute(value, axis, [(i, i ^ mask) for i in range(lax.axis_size(axis))])


def spread(whole, halves, axis):
    n = lax.axis_size(axis)
    if n != 4:
        return [whole] + [swap(whole, axis, k) for k in range(1, n)]
    seconds = [swap(half, axis, 2) for half in halves]
    first = swap(whole, axis, 1)
    middle = lax.ppermute(whole, axis, [(1, 2), (2, 1)])
    ends = [lax.ppermute(second, axis, [(1, 0), (2, 3)]) for second in seconds]
    return [whole, first, middle, *seconds, *ends]


def split(x):
    high = x.astype(BF16)
    return high, (x - high.astype(F32)).astype(BF16)


def dot3(ah, al, bh, bl, dims=((1,), (0,))):
    d = functools.partial(lax.dot_general, dimension_numbers=(dims, ((), ())), preferred_element_type=F32)
    return d(ah, bh) + (d(ah, bl) + d(al, bh))


def dotf(a, b, dims=((1,), (0,))):
    return dot3(*split(a), *split(b), dims)


def bit_of(level):
    return (lax.axis_index("row") >> level) & 1


def place(pieces, start, rows, out):
    mine = lax.axis_index("col")
    span = pl.ds(start, rows)

    def put(k, *parts):
        to = pl.ds(pl.multiple_of((mine ^ k) * rows, rows), rows)
        size = out.shape[1] // len(parts)
        for i, part in enumerate(parts):
            out[to, pl.ds(i * size, size)] = part[span, :]

    if out.shape[0] == rows * len(pieces):
        for k, piece in enumerate(pieces):
            put(k, piece)
        return
    put(0, pieces[0])
    put(1, pieces[1])
    put(2, *pieces[3:5])
    inner = (mine == 1) | (mine == 2)
    pl.when(inner)(lambda: put(3, pieces[2]))
    pl.when(jnp.logical_not(inner))(lambda: put(3, *pieces[5:7]))


def pack(*refs):
    *sources, whole, left, right, sems = refs
    size = left.shape[1]
    copies, start = [], 0
    for source in sources:
        to = pl.ds(start, source.shape[0])
        for half, target in ((pl.ds(0, 2 * size), whole), (pl.ds(0, size), left), (pl.ds(size, size), right)):
            copies.append(pltpu.make_async_copy(source.at[:, half], target.at[to], sems.at[len(copies)]))
            copies[-1].start()
        start += source.shape[0]
    for c in copies:
        c.wait()


def token(out):
    out[...] = jnp.zeros_like(out)


def tree_blocks(n, start, rows, *refs):
    pieces, outs, odd = refs[:n], refs[n:-1], refs[-1]
    for level, out in enumerate(outs):
        place(pieces, pl.multiple_of(start + bit_of(level) * rows, rows), rows, out)
    mine = lax.axis_index("col")
    for k in range(odd.shape[0] // rows):
        odd[pl.ds(k * rows, rows), :] = outs[1][pl.ds(pl.multiple_of((mine ^ (2 * k + 1)) * rows, rows), rows), :]


def even_rows(n, start, rows, *refs):
    span = pl.ds(pl.multiple_of(start + bit_of(1) * rows, rows), rows)
    out = refs[-1]
    if n == 4:
        whole, left, right = refs[:-1]
        size = left.shape[1]
        out[:rows, :] = whole[span, :]
        out[rows:, :size], out[rows:, size:] = left[span, :], right[span, :]
    else:
        for k, piece in enumerate(refs[:-1]):
            out[pl.ds(k * rows, rows), :] = piece[span, :]


def level_factors(level, rows, own, *refs):
    width = own.shape[0]
    if len(refs) == 3:
        far, fh, fl = refs
    else:
        even, odd, fh, fl, far = refs
        mine = lax.axis_index("col")
        for k in range(width // rows):
            to = pl.ds(pl.multiple_of((mine ^ k) * rows, rows), rows)
            far[to, :] = (odd if k % 2 else even)[pl.ds(k // 2 * rows, rows), :]

    @pl.when(bit_of(level) == 0)
    def _():
        s, y = own[...], far[...]
        fh[:, :width], fl[:, :width] = split(s.T)
        fh[:, width:], fl[:, width:] = split(dotf(y, s).T)

    @pl.when(bit_of(level) == 1)
    def _():
        y, s = own[...], far[...]
        ys = dotf(y, s, ((1,), (1,)))
        fh[:, width:], fl[:, width:] = split(ys)
        fh[:, :width], fl[:, :width] = split(dotf(ys, y, ((1,), (1,))))


def load(c, out, high, low, buffer, sems):
    size = buffer.shape[2]
    copies = []
    for k in range(buffer.shape[0]):
        copies.append(pltpu.make_async_copy(c.at[:, pl.ds(k * size, size)], buffer.at[k], sems.at[k]))
        copies[-1].start()
    for k, copy in enumerate(copies):
        at = pl.ds(k * size, size)
        copy.wait()
        out[:, at] = buffer[k]
        high[:, at], low[:, at] = split(buffer[k])


def leaf_factors(n, vr, tr, *refs):
    pieces, (vth, vtl, ph, plo), (v, t) = refs[:n], refs[n:n + 4], refs[n + 4:]
    place(pieces, 0, vr, v)
    place(pieces, vr, tr, t)
    full = v[...]
    vth[...], vtl[...] = split(full.T)
    ph[...], plo[...] = split(dotf(full, t[...], ((1,), (1,))))


def leaf_apply(starts, c, ch, cl, vth, vtl, ph, plo, *outs):
    for k, start in enumerate(starts):
        top, *others = outs[k * len(outs) // len(starts):(k + 1) * len(outs) // len(starts)]
        width, size = top.shape
        at = pl.ds(start, size)
        h, l = split(dot3(vth[...], vtl[...], ch[:, at], cl[:, at]))
        if len(others) == 2:
            others[0][...], others[1][...] = h, l
            top[...] = c[:width, at] - dot3(ph[:width, :], plo[:width, :], h, l)
        else:
            change = dot3(ph[...], plo[...], h, l)
            top[...] = c[:width, at] - change[:width]
            others[0][...] = c[width:, at] - change[width:]


def rest_apply(start, c, ph, plo, ih, il, out):
    width, size = ih.shape
    out[...] = c[width:, pl.ds(start, size)] - dot3(ph[width:, :], plo[width:, :], ih[...], il[...])


def level_result(start, own, far, fh, fl, size):
    width = own.shape[0]
    mine, other = own[:, pl.ds(start, size)], far[:, pl.ds(start, size)]
    change = dot3(fh[:, :width], fl[:, :width], *split(mine)) + dot3(fh[:, width:], fl[:, width:], *split(other))
    return mine - change


def level_apply(start, own, far, fh, fl, out):
    out[...] = level_result(start, own, far, fh, fl, out.shape[1])


def store(sources, out, top, left, sems, first=0):
    copies = []
    for k, source in enumerate(sources):
        rows, size = source.shape
        to = out.at[pl.ds(top, rows), pl.ds(left + k * size, size)]
        copies.append(pltpu.make_async_copy(source, to, sems.at[first + k]))
        copies[-1].start()
    return copies


def early_store(*refs):
    *sources, out, sems = refs
    lower, upper = sources[:CHUNKS], sources[CHUNKS:]
    for copy in store(lower, out, out.shape[0] - lower[0].shape[0], 0, sems) + store(upper, out, 0, 0, sems, CHUNKS):
        copy.wait()


def own_part(own, fh, fl, out):
    width = own.shape[0]
    mine = own[...]
    out[...] = mine - dot3(fh[:, :width], fl[:, :width], *split(mine))


def last_apply(part, far, fh, fl, *refs):
    *sources, _, out, buffer, sems = refs
    width, size = part.shape
    start = out.shape[1] - size
    copies = store(sources, out, 0, start - len(sources) * size, sems)
    half = size // 2
    for k in range(2):
        at = pl.ds(k * half, half)
        buffer[:, at] = part[:, at] - dot3(fh[:, width:], fl[:, width:], *split(far[:, at]))
        to = out.at[pl.ds(0, width), pl.ds(start + k * half, half)]
        copies.append(pltpu.make_async_copy(buffer.at[:, at], to, sems.at[len(sources) + k]))
        copies[-1].start()
    for copy in copies:
        copy.wait()


def per_device(trailing, leaf_v, leaf_t, tree_y, tree_t):
    height, columns = trailing.shape
    width = leaf_v.shape[1]
    vr, tr = leaf_v.shape[0], leaf_t.shape[0]
    depth = lax.axis_size("row").bit_length() - 1
    part = columns // CHUNKS
    steps = columns // STEP
    block, block16 = pltpu.VMEM((width, width), F32), lambda *shape: pltpu.VMEM(shape, BF16)

    rows = vr + 3 * tr
    whole, *halves = call(
        pack,
        "pack",
        (leaf_v, leaf_t, tree_t, tree_y),
        [pltpu.VMEM((rows, width), F32)] + [pltpu.VMEM((rows, width // 2), F32)] * 2,
        [pltpu.SemaphoreType.DMA((12,))],
        hbm_in=range(4),
    )
    pieces = spread(whole, halves, "col")
    n = lax.axis_size("col")
    some = [pieces[0], *pieces[3:5]] if n == 4 else pieces[0::2]
    half = pltpu.VMEM((width // 2, width), F32)
    (even,) = call(functools.partial(even_rows, n, vr + tr, tr), "even_rows", some, [half])
    even = swap(even, "row", 2)
    c, ch, cl = call(
        load,
        "load",
        (trailing,),
        [pltpu.VMEM((height, columns), F32)] + [block16(height, columns)] * 2,
        [pltpu.VMEM((steps, height, STEP), F32), pltpu.SemaphoreType.DMA((steps,))],
        hbm_in=(0,),
        after=pieces[3:5],
    )
    *owns, odd = call(
        functools.partial(tree_blocks, len(pieces), vr + tr, tr), "tree_blocks", pieces, [block] * depth + [half], after=[ch]
    )
    odd = swap(odd, "row", 2)
    (arrived,) = call(token, "arrived", (), [pltpu.VMEM((8, 128), F32)], after=[odd], size=2 * 10**9)
    factors = [
        call(
            functools.partial(level_factors, level, tr),
            f"factors{level}",
            (owns[level], *([even, odd] if level == 1 else [swap(owns[level], "row", 1 << level)])),
            [block16(width, 2 * width)] * 2,
            [block] * (level == 1),
        )
        for level in range(depth)
    ]
    vth, vtl, ph, plo = call(
        functools.partial(leaf_factors, len(pieces), vr, tr),
        "leaf_factors",
        pieces,
        [block16(width, height)] * 2 + [block16(height, width)] * 2,
        [pltpu.VMEM((height, width), F32), block],
        after=[even],
    )

    made = [[] for _ in range(depth - 1)]
    sent = [[] for _ in range(depth - 1)]
    pending = {}

    def advance(level, own, far, at, waits):
        (chunk,) = call(
            functools.partial(level_apply, at),
            f"level{level}",
            (own, far, *factors[level]),
            [pltpu.VMEM((width, part), F32)],
            after=waits,
        )
        made[level].append(chunk)
        sent[level].append(swap(chunk, "row", 2 << level))

    def later(k):
        for level in range(1, depth - 1):
            waits = [made[0][1]] if level == 1 and k == 0 else []
            if level == 1 and k == 1:
                waits = [factors[-1][0]]
            if level == depth - 2 and k >= 2:
                waits = done[k - 2:k - 1]
            advance(level, made[level - 1][k], sent[level - 1][k], 0, waits)

    done, rests, tops, fars = [], {}, {}, {}

    def make_leaf(k):
        if k in tops:
            return
        above, below = pltpu.VMEM((width, part), F32), pltpu.VMEM((height - width, part), F32)
        ks = LEAVES.get(k, (k,))
        outs = call(
            functools.partial(leaf_apply, [j * part for j in ks]),
            f"leaf_{k}",
            (c, ch, cl, vth, vtl, ph, plo),
            [above, *([block16(width, part)] * 2 if k < 2 else [below])] * len(ks),
            after=[tops[0]] if k == 1 else made[0][k - 2:k - 1] if k else (),
        )
        if k < 2:
            outs = (outs[0], *call(
                functools.partial(rest_apply, k * part), f"rest_{k}", (c, ph, plo, *outs[1:]), [below], after=made[0][k:k + 1]
            ))
        for j, top, rest in zip(ks, outs[0::2], outs[1::2]):
            tops[j], rests[j], fars[j] = top, rest, swap(top, "row", 1)

    def first_level(k):
        waits = made[min(1, depth - 2)][k - 2:k - 1] if k >= 2 else [arrived] * (1 - k)
        advance(0, tops[k], fars[k], 0, waits)

    make_leaf(0)
    make_leaf(1)
    first_level(0)
    first_level(1)
    make_leaf(2)
    for k in range(CHUNKS):
        later(k)
        if k + 2 < CHUNKS:
            first_level(k + 2)
        if k + 3 < CHUNKS:
            make_leaf(k + 3)
        if k < CHUNKS - 1:
            done += call(
                functools.partial(level_apply, 0),
                "last",
                (made[-1][k], sent[-1][k], *factors[-1]),
                [pltpu.VMEM((width, part), F32)],
            )
    whole = jax.ShapeDtypeStruct((height, columns), F32)
    sems, kept = pltpu.SemaphoreType.DMA((2 * CHUNKS,)), CHUNKS - 3
    early = [rests[k] for k in range(CHUNKS)] + done[:kept]
    (out,) = call(early_store, "early_store", early, [whole], [sems], hbm_out=(0,))
    late = done[kept:]
    (mine,) = call(own_part, "own_part", (made[-1][-1], *factors[-1]), [pltpu.VMEM((width, part), F32)])
    (out,) = call(
        last_apply,
        "finish",
        (mine, sent[-1][-1], *factors[-1], *late, out),
        [whole],
        [pltpu.VMEM((width, part), F32), sems],
        hbm_in=(4 + len(late),),
        hbm_out=(0,),
        alias={4 + len(late): 0},
    )
    return out


def solution(mesh):
    return jax.shard_map(
        per_device,
        mesh=mesh,
        in_specs=(
            P("row", "col"),
            P(("row", "col"), None),
            P(("row", "col"), None),
            P(("row", "col"), None),
            P(("row", "col"), None),
        ),
        out_specs=P("row", "col"),
        check_vma=False,
    )
```

```python
import functools

import jax
import jax.numpy as jnp
from jax import lax
from jax.experimental import pallas as pl
from jax.experimental.pallas import tpu as pltpu
from jax.sharding import PartitionSpec as P

CHUNKS = 8
LEAVES = {2: (2, 4), 3: (3, 5)}
STEP = 512
F32, BF16 = jnp.float32, jnp.bfloat16
VMEM = pl.BlockSpec(memory_space=pltpu.VMEM)
ANY = pl.BlockSpec(memory_space=pl.ANY)
TOKEN = pltpu.VMEM((8, 128), F32)


def call(kernel, name, args, outs, scratch=(), hbm_in=(), hbm_out=(), alias=None, after=(), size=1000):
    count, waits = len(args), len(after)

    def body(*refs):
        kernel(*refs[:count], *refs[count + waits:])

    spaces = [pltpu.HBM if k in hbm_in else pltpu.VMEM for k in range(count)] + [pltpu.VMEM] * waits
    return pl.pallas_call(
        body,
        out_shape=[jax.ShapeDtypeStruct(o.shape, o.dtype) if k in hbm_out else o for k, o in enumerate(outs)],
        in_specs=[ANY if s is pltpu.HBM else VMEM for s in spaces],
        out_specs=[ANY if k in hbm_out else VMEM for k in range(len(outs))],
        scratch_shapes=list(scratch),
        input_output_aliases=alias or {},
        compiler_params=pltpu.CompilerParams(vmem_limit_bytes=20 << 20),
        cost_estimate=pl.CostEstimate(flops=size, bytes_accessed=1000, transcendentals=0),
        name=name,
    )(*map(pltpu.with_memory_space_constraint, (*args, *after), spaces))


def swap(value, axis, mask):
    return lax.ppermute(value, axis, [(i, i ^ mask) for i in range(lax.axis_size(axis))])


def spread(whole, halves, axis):
    n = lax.axis_size(axis)
    if n != 4:
        return [whole] + [swap(whole, axis, k) for k in range(1, n)]
    seconds = [swap(half, axis, 2) for half in halves]
    first = swap(whole, axis, 1)
    middle = lax.ppermute(whole, axis, [(1, 2), (2, 1)])
    ends = [lax.ppermute(second, axis, [(1, 0), (2, 3)]) for second in seconds]
    return [whole, first, middle, *seconds, *ends]


def split(x):
    high = x.astype(BF16)
    return high, (x - high.astype(F32)).astype(BF16)


def dot3(ah, al, bh, bl, dims=((1,), (0,))):
    d = functools.partial(lax.dot_general, dimension_numbers=(dims, ((), ())), preferred_element_type=F32)
    return d(ah, bh) + (d(ah, bl) + d(al, bh))


def dotf(a, b, dims=((1,), (0,))):
    return dot3(*split(a), *split(b), dims)


def bit_of(level):
    return (lax.axis_index("row") >> level) & 1


def place(pieces, start, rows, out):
    mine = lax.axis_index("col")
    span = pl.ds(start, rows)

    def put(k, *parts):
        to = pl.ds(pl.multiple_of((mine ^ k) * rows, rows), rows)
        size = out.shape[1] // len(parts)
        for i, part in enumerate(parts):
            out[to, pl.ds(i * size, size)] = part[span, :]

    if out.shape[0] == rows * len(pieces):
        for k, piece in enumerate(pieces):
            put(k, piece)
        return
    put(0, pieces[0])
    put(1, pieces[1])
    put(2, *pieces[3:5])
    inner = (mine == 1) | (mine == 2)
    pl.when(inner)(lambda: put(3, pieces[2]))
    pl.when(jnp.logical_not(inner))(lambda: put(3, *pieces[5:7]))


def pack(*refs):
    *sources, whole, left, right, sems = refs
    size = left.shape[1]
    copies, start = [], 0
    for source in sources:
        to = pl.ds(start, source.shape[0])
        for half, target in ((pl.ds(0, 2 * size), whole), (pl.ds(0, size), left), (pl.ds(size, size), right)):
            copies.append(pltpu.make_async_copy(source.at[:, half], target.at[to], sems.at[len(copies)]))
            copies[-1].start()
        start += source.shape[0]
    for c in copies:
        c.wait()


def token(out):
    out[...] = jnp.zeros_like(out)


def tree_blocks(n, start, rows, *refs):
    pieces, outs, odd = refs[:n], refs[n:-1], refs[-1]
    for level, out in enumerate(outs):
        place(pieces, pl.multiple_of(start + bit_of(level) * rows, rows), rows, out)
    mine = lax.axis_index("col")
    for k in range(odd.shape[0] // rows):
        odd[pl.ds(k * rows, rows), :] = outs[1][pl.ds(pl.multiple_of((mine ^ (2 * k + 1)) * rows, rows), rows), :]


def even_rows(n, start, rows, *refs):
    span = pl.ds(pl.multiple_of(start + bit_of(1) * rows, rows), rows)
    out = refs[-1]
    if n == 4:
        whole, left, right = refs[:-1]
        size = left.shape[1]
        out[:rows, :] = whole[span, :]
        out[rows:, :size], out[rows:, size:] = left[span, :], right[span, :]
    else:
        for k, piece in enumerate(refs[:-1]):
            out[pl.ds(k * rows, rows), :] = piece[span, :]


def level_factors(level, rows, own, *refs):
    width = own.shape[0]
    if len(refs) == 3:
        far, fh, fl = refs
    else:
        even, odd, fh, fl, far = refs
        mine = lax.axis_index("col")
        for k in range(width // rows):
            to = pl.ds(pl.multiple_of((mine ^ k) * rows, rows), rows)
            far[to, :] = (odd if k % 2 else even)[pl.ds(k // 2 * rows, rows), :]

    @pl.when(bit_of(level) == 0)
    def _():
        s, y = own[...], far[...]
        fh[:, :width], fl[:, :width] = split(s.T)
        fh[:, width:], fl[:, width:] = split(dotf(y, s).T)

    @pl.when(bit_of(level) == 1)
    def _():
        y, s = own[...], far[...]
        ys = dotf(y, s, ((1,), (1,)))
        fh[:, width:], fl[:, width:] = split(ys)
        fh[:, :width], fl[:, :width] = split(dotf(ys, y, ((1,), (1,))))


def load(c, out, high, low, buffer, sems):
    size = buffer.shape[2]
    copies = []
    for k in range(buffer.shape[0]):
        copies.append(pltpu.make_async_copy(c.at[:, pl.ds(k * size, size)], buffer.at[k], sems.at[k]))
        copies[-1].start()
    for k, copy in enumerate(copies):
        at = pl.ds(k * size, size)
        copy.wait()
        out[:, at] = buffer[k]
        high[:, at], low[:, at] = split(buffer[k])


def leaf_factors(n, vr, tr, *refs):
    pieces, (vth, vtl, ph, plo), (v, t) = refs[:n], refs[n:n + 4], refs[n + 4:]
    place(pieces, 0, vr, v)
    place(pieces, vr, tr, t)
    full = v[...]
    vth[...], vtl[...] = split(full.T)
    ph[...], plo[...] = split(dotf(full, t[...], ((1,), (1,))))


def leaf_apply(starts, c, ch, cl, vth, vtl, ph, plo, *outs):
    for k, start in enumerate(starts):
        top, *others = outs[k * len(outs) // len(starts):(k + 1) * len(outs) // len(starts)]
        width, size = top.shape
        at = pl.ds(start, size)
        h, l = split(dot3(vth[...], vtl[...], ch[:, at], cl[:, at]))
        if len(others) == 2:
            others[0][...], others[1][...] = h, l
            top[...] = c[:width, at] - dot3(ph[:width, :], plo[:width, :], h, l)
        else:
            change = dot3(ph[...], plo[...], h, l)
            top[...] = c[:width, at] - change[:width]
            others[0][...] = c[width:, at] - change[width:]


def rest_apply(start, c, ph, plo, ih, il, out):
    width, size = ih.shape
    out[...] = c[width:, pl.ds(start, size)] - dot3(ph[width:, :], plo[width:, :], ih[...], il[...])


def level_result(start, own, far, fh, fl, size):
    width = own.shape[0]
    mine, other = own[:, pl.ds(start, size)], far[:, pl.ds(start, size)]
    change = dot3(fh[:, :width], fl[:, :width], *split(mine)) + dot3(fh[:, width:], fl[:, width:], *split(other))
    return mine - change


def level_apply(start, own, far, fh, fl, out):
    out[...] = level_result(start, own, far, fh, fl, out.shape[1])


def store(sources, out, top, left, sems, first=0):
    copies = []
    for k, source in enumerate(sources):
        rows, size = source.shape
        to = out.at[pl.ds(top, rows), pl.ds(left + k * size, size)]
        copies.append(pltpu.make_async_copy(source, to, sems.at[first + k]))
        copies[-1].start()
    return copies


def early_store(*refs):
    *sources, out, sems = refs
    lower, upper = sources[:CHUNKS], sources[CHUNKS:]
    for copy in store(lower, out, out.shape[0] - lower[0].shape[0], 0, sems) + store(upper, out, 0, 0, sems, CHUNKS):
        copy.wait()


def own_part(own, fh, fl, out):
    width = own.shape[0]
    mine = own[...]
    out[...] = mine - dot3(fh[:, :width], fl[:, :width], *split(mine))


def last_apply(part, far, fh, fl, *refs):
    *sources, _, out, buffer, sems = refs
    width, size = part.shape
    start = out.shape[1] - size
    copies = store(sources, out, 0, start - len(sources) * size, sems)
    half = size // 2
    for k in range(2):
        at = pl.ds(k * half, half)
        buffer[:, at] = part[:, at] - dot3(fh[:, width:], fl[:, width:], *split(far[:, at]))
        to = out.at[pl.ds(0, width), pl.ds(start + k * half, half)]
        copies.append(pltpu.make_async_copy(buffer.at[:, at], to, sems.at[len(sources) + k]))
        copies[-1].start()
    for copy in copies:
        copy.wait()


def per_device(trailing, leaf_v, leaf_t, tree_y, tree_t):
    height, columns = trailing.shape
    width = leaf_v.shape[1]
    vr, tr = leaf_v.shape[0], leaf_t.shape[0]
    depth = lax.axis_size("row").bit_length() - 1
    part = columns // CHUNKS
    steps = columns // STEP
    block, block16 = pltpu.VMEM((width, width), F32), lambda *shape: pltpu.VMEM(shape, BF16)

    rows = vr + 3 * tr
    whole, *halves = call(
        pack,
        "pack",
        (leaf_v, leaf_t, tree_t, tree_y),
        [pltpu.VMEM((rows, width), F32)] + [pltpu.VMEM((rows, width // 2), F32)] * 2,
        [pltpu.SemaphoreType.DMA((12,))],
        hbm_in=range(4),
    )
    pieces = spread(whole, halves, "col")
    n = lax.axis_size("col")
    some = [pieces[0], *pieces[3:5]] if n == 4 else pieces[0::2]
    half = pltpu.VMEM((width // 2, width), F32)
    (even,) = call(functools.partial(even_rows, n, vr + tr, tr), "even_rows", some, [half])
    even = swap(even, "row", 2)
    c, ch, cl = call(
        load,
        "load",
        (trailing,),
        [pltpu.VMEM((height, columns), F32)] + [block16(height, columns)] * 2,
        [pltpu.VMEM((steps, height, STEP), F32), pltpu.SemaphoreType.DMA((steps,))],
        hbm_in=(0,),
        after=pieces[3:5],
    )
    *owns, odd = call(
        functools.partial(tree_blocks, len(pieces), vr + tr, tr), "tree_blocks", pieces, [block] * depth + [half], after=[ch, even]
    )
    odd = swap(odd, "row", 2)
    (arrived,) = call(token, "arrived", (), [pltpu.VMEM((8, 128), F32)], after=[odd], size=2 * 10**9)
    factors = [
        call(
            functools.partial(level_factors, level, tr),
            f"factors{level}",
            (owns[level], *([even, odd] if level == 1 else [swap(owns[level], "row", 1 << level)])),
            [block16(width, 2 * width)] * 2,
            [block] * (level == 1),
        )
        for level in range(depth)
    ]
    vth, vtl, ph, plo = call(
        functools.partial(leaf_factors, len(pieces), vr, tr),
        "leaf_factors",
        pieces,
        [block16(width, height)] * 2 + [block16(height, width)] * 2,
        [pltpu.VMEM((height, width), F32), block],
        after=[even],
    )

    made = [[] for _ in range(depth - 1)]
    sent = [[] for _ in range(depth - 1)]
    pending = {}

    def advance(level, own, far, at, waits):
        (chunk,) = call(
            functools.partial(level_apply, at),
            f"level{level}",
            (own, far, *factors[level]),
            [pltpu.VMEM((width, part), F32)],
            after=waits,
        )
        made[level].append(chunk)
        sent[level].append(swap(chunk, "row", 2 << level))

    def later(k):
        for level in range(1, depth - 1):
            waits = [made[0][1]] if level == 1 and k == 0 else []
            if level == 1 and k == 1:
                waits = [factors[-1][0]]
            if level == depth - 2 and k >= 2:
                waits = done[k - 2:k - 1]
            advance(level, made[level - 1][k], sent[level - 1][k], 0, waits)

    done, rests, tops, fars = [], {}, {}, {}

    def make_leaf(k):
        if k in tops:
            return
        above, below = pltpu.VMEM((width, part), F32), pltpu.VMEM((height - width, part), F32)
        ks = LEAVES.get(k, (k,))
        outs = call(
            functools.partial(leaf_apply, [j * part for j in ks]),
            f"leaf_{k}",
            (c, ch, cl, vth, vtl, ph, plo),
            [above, *([block16(width, part)] * 2 if k < 2 else [below])] * len(ks),
            after=[tops[0], factors[0][0]] if k == 1 else made[0][k - 2:k - 1] if k else (),
        )
        if k < 2:
            outs = (outs[0], *call(
                functools.partial(rest_apply, k * part), f"rest_{k}", (c, ph, plo, *outs[1:]), [below], after=made[0][k:k + 1]
            ))
        for j, top, rest in zip(ks, outs[0::2], outs[1::2]):
            tops[j], rests[j], fars[j] = top, rest, swap(top, "row", 1)

    def first_level(k):
        waits = made[min(1, depth - 2)][k - 2:k - 1] if k >= 2 else [arrived] * (1 - k)
        advance(0, tops[k], fars[k], 0, waits)

    make_leaf(0)
    make_leaf(1)
    first_level(0)
    first_level(1)
    make_leaf(2)
    for k in range(CHUNKS):
        later(k)
        if k + 2 < CHUNKS:
            first_level(k + 2)
        if k + 3 < CHUNKS:
            make_leaf(k + 3)
        if k < CHUNKS - 1:
            done += call(
                functools.partial(level_apply, 0),
                "last",
                (made[-1][k], sent[-1][k], *factors[-1]),
                [pltpu.VMEM((width, part), F32)],
            )
    whole = jax.ShapeDtypeStruct((height, columns), F32)
    sems, kept = pltpu.SemaphoreType.DMA((2 * CHUNKS,)), CHUNKS - 3
    early = [rests[k] for k in range(CHUNKS)] + done[:kept]
    (out,) = call(early_store, "early_store", early, [whole], [sems], hbm_out=(0,))
    late = done[kept:]
    (mine,) = call(own_part, "own_part", (made[-1][-1], *factors[-1]), [pltpu.VMEM((width, part), F32)])
    (out,) = call(
        last_apply,
        "finish",
        (mine, sent[-1][-1], *factors[-1], *late, out),
        [whole],
        [pltpu.VMEM((width, part), F32), sems],
        hbm_in=(4 + len(late),),
        hbm_out=(0,),
        alias={4 + len(late): 0},
    )
    return out


def solution(mesh):
    return jax.shard_map(
        per_device,
        mesh=mesh,
        in_specs=(
            P("row", "col"),
            P(("row", "col"), None),
            P(("row", "col"), None),
            P(("row", "col"), None),
            P(("row", "col"), None),
        ),
        out_specs=P("row", "col"),
        check_vma=False,
    )
```
